32 devices in a mesh: section: 8 (over z, x), fsdp: 4 (over y, core).
Axes of the slice: x: 2, y: 2, z: 4, core: 2. Of those that a mesh axis runs over, the one named last changes fastest.
Arguments:
- out_grad: bfloat16 [8, 2, 256, 3072], P('section', None, 'fsdp'), may hold values from -1.5 to 1.5
- expert_ids: int32 [8, 2, 256, 2], P('section', None, 'fsdp'), may hold values from 0 to 7, as said below
- route_weight: bfloat16 [8, 2, 256], P('section', None, 'fsdp'), may hold values from 0.099609375 to 0.8984375
- gate_pre: bfloat16 [8, 2, 128, 8192], P('section', None, None, 'fsdp'), may hold values from -6 to 6
- up_pre: bfloat16 [8, 2, 128, 8192], P('section', None, None, 'fsdp'), may hold values from -6 to 6
- w_gate: bfloat16 [8, 3072, 8192], P('section', None, 'fsdp'), may hold values from -0.109375 to 0.109375
- w_up: bfloat16 [8, 3072, 8192], P('section', None, 'fsdp'), may hold values from -0.109375 to 0.109375
- w_down: bfloat16 [8, 8192, 3072], P('section', 'fsdp'), may hold values from -0.0625 to 0.0625
Outputs:
- prev_grad: bfloat16 [8, 2, 256, 3072], P('section', None, 'fsdp')
- route_grad: float32 [8, 2, 256], P('section', None, 'fsdp')
The draws below stay inside these ranges and needn't reach their ends.
Inputs may be any that keep to these rules, and one draw needn't show every extreme that they name: `expert_ids`: each token names two different experts. Among the 64 tokens of one aligned block (one index of fsdp, one microbatch) at most 32 name expert 0; in every section and microbatch some block has exactly 32, and for each microbatch every block of some section has exactly 32.
All inputs are finite; a program needn't handle non-finite values.
Results may differ from the reference program's by a relative error of at most 0.01.
Values may be sent and summed in bfloat16 or wider, within the bound.
A program may use at most 128 MiB of HBM per device.

```python
import jax
import jax.numpy as jnp
from jax import lax

D = 3072
FF = 8192
MICRO = 2
TOK_MB = 64
CAP = 32
ROWS = 128
TOKENS = 256
SECTIONS = 8
N_FSDP = 4


def draw_expert_ids(key, part):
    blocks = TOKENS // TOK_MB
    keys = jax.random.split(key, 7)
    counts = jax.random.randint(keys[0], (SECTIONS, MICRO, blocks), CAP // 4, CAP + 1)
    full_block = jax.random.randint(keys[1], (SECTIONS, MICRO, 1), 0, blocks)
    full_section = jax.random.randint(keys[2], (1, MICRO, 1), 0, SECTIONS)
    block_iota = lax.broadcasted_iota(jnp.int32, (SECTIONS, MICRO, blocks), 2)
    section_iota = lax.broadcasted_iota(jnp.int32, (SECTIONS, MICRO, blocks), 0)
    counts = jnp.where((block_iota == full_block) | (section_iota == full_section), CAP, counts)
    perm_keys = jax.random.split(keys[3], SECTIONS * MICRO * blocks)

    def shuffled(one_key):
        return jax.random.permutation(one_key, TOK_MB)
    ranks = jax.vmap(shuffled)(perm_keys).reshape(SECTIONS, MICRO, blocks, TOK_MB)
    routed = ranks < counts[..., None]
    shape = (SECTIONS, MICRO, blocks, TOK_MB)
    other = jax.random.randint(keys[4], shape, 1, 8)
    column = jax.random.randint(keys[5], shape, 0, 2)
    offset = jax.random.randint(keys[6], shape, 1, 7)
    second = 1 + (other - 1 + offset) % 7
    first_col = jnp.where(routed, jnp.where(column == 0, 0, other), other)
    second_col = jnp.where(routed, jnp.where(column == 0, other, 0), second)
    paired = jnp.stack([first_col, second_col], axis=-1)
    return paired.reshape(SECTIONS, MICRO, TOKENS, 2).astype(jnp.int32)


def block_levels(rng, dims, cuts, least, largest):
    gain = 1.0
    for axis_at, blocks in cuts:
        heights = jax.random.uniform(jax.random.fold_in(jax.random.fold_in(rng, 6), axis_at), (blocks,), jnp.float32, least / len(cuts), largest / len(cuts))
        gain = gain * jnp.repeat(jnp.exp(heights), dims[axis_at] // blocks).reshape((-1,) + (1,) * (len(dims) - 1 - axis_at))
    return gain


def normal_values(key, extent, scale, limit, cuts=(), dtype=jnp.bfloat16):
    result = scale * jax.random.normal(key, extent, jnp.float32)
    if cuts:
        result = result * block_levels(key, extent, cuts, -0.22, 0.18)
    return jnp.clip(result, -limit, limit).astype(dtype)


def setup_inputs(seed: int = 0) -> dict:
    key_list = jax.random.split(jax.random.key(seed), 9)
    return {
        "out_grad": normal_values(key_list[0], (SECTIONS, MICRO, TOKENS, D), 0.25, 1.5, ((0, 8), (2, 4))),
        "expert_ids": draw_expert_ids(jax.random.fold_in(key_list[8], 71), 0),
        "route_weight": jnp.clip(0.099609375 + 0.7988281 * jax.random.uniform(key_list[2], (SECTIONS, MICRO, TOKENS), jnp.float32) ** block_levels(key_list[2], (SECTIONS, MICRO, TOKENS), ((0, 8), (2, 4)), -0.2, 0.2), 0.099609375, 0.8984375).astype(jnp.bfloat16),
        "gate_pre": normal_values(key_list[3], (SECTIONS, MICRO, ROWS, FF), 1.0, 6.0, ((0, 8), (3, 4))),
        "up_pre": normal_values(key_list[4], (SECTIONS, MICRO, ROWS, FF), 1.0, 6.0, ((0, 8), (3, 4))),
        "w_gate": normal_values(key_list[5], (SECTIONS, D, FF), D ** -0.5, 0.109375, ((0, 8), (2, 4))),
        "w_up": normal_values(key_list[6], (SECTIONS, D, FF), D ** -0.5, 0.109375, ((0, 8), (2, 4))),
        "w_down": normal_values(key_list[7], (SECTIONS, FF, D), FF ** -0.5, 0.0625, ((0, 8), (1, 4))),
    }


def one_block(dy, ids, weight, gate, up, wg, wu, wd):
    blocks = TOKENS // TOK_MB
    routed = jnp.any(ids == 0, axis=-1)
    routed_blocks = routed.reshape(blocks, TOK_MB).astype(jnp.int32)
    order = jnp.cumsum(routed_blocks, axis=1) - 1
    base = (lax.broadcasted_iota(jnp.int32, (blocks, TOK_MB), 0) * CAP).astype(jnp.int32)
    row_index = (base + order).reshape(TOKENS).astype(jnp.int32)
    target = jnp.where(routed, row_index, ROWS).astype(jnp.int32)
    rows_dy = jnp.zeros((ROWS + 1, D), jnp.bfloat16).at[target].set(dy)[:ROWS]
    rows_weight = jnp.zeros((ROWS + 1,), jnp.bfloat16).at[target].set(weight)[:ROWS]
    q = lax.dot_general(rows_dy, wd, (((1,), (1,)), ((), ())), preferred_element_type=jnp.float32)
    g = gate.astype(jnp.float32)
    u = up.astype(jnp.float32)
    sg = jax.nn.sigmoid(g)
    hidden = g * sg * u
    dh = rows_weight.astype(jnp.float32)[:, None] * q
    d_gate = (dh * u * sg * (1.0 + g * (1.0 - sg))).astype(jnp.bfloat16)
    d_up = (dh * g * sg).astype(jnp.bfloat16)
    width = FF // N_FSDP
    part_route = jnp.sum((hidden * q).reshape(ROWS, N_FSDP, width), axis=2).astype(jnp.bfloat16)
    part_route = lax.optimization_barrier(part_route)
    row_route = jnp.sum(part_route.astype(jnp.float32), axis=1)
    dg3 = d_gate.reshape(ROWS, N_FSDP, width).astype(jnp.float32)
    du3 = d_up.reshape(ROWS, N_FSDP, width).astype(jnp.float32)
    wg3 = wg.reshape(D, N_FSDP, width).astype(jnp.float32)
    wu3 = wu.reshape(D, N_FSDP, width).astype(jnp.float32)
    part_back = jnp.einsum("rnf,dnf->nrd", dg3, wg3) + jnp.einsum("rnf,dnf->nrd", du3, wu3)
    part_back = lax.optimization_barrier(part_back.astype(jnp.bfloat16))
    row_back = jnp.sum(part_back.astype(jnp.float32), axis=0)
    safe = jnp.where(routed, row_index, 0).astype(jnp.int32)
    back_tok = jnp.where(routed[:, None], row_back[safe], jnp.float32(0.0))
    route_tok = jnp.where(routed, row_route[safe], jnp.float32(0.0))
    input_grad = (dy.astype(jnp.float32) + back_tok).astype(jnp.bfloat16)
    return input_grad, route_tok


def reference(out_grad, expert_ids, route_weight, gate_pre, up_pre, w_gate, w_up, w_down):
    inputs = []
    routes = []
    for section_no in range(SECTIONS):
        section_inputs = []
        section_routes = []
        for micro_no in range(MICRO):
            grad_in, grad_route = one_block(out_grad[section_no, micro_no], expert_ids[section_no, micro_no], route_weight[section_no, micro_no], gate_pre[section_no, micro_no], up_pre[section_no, micro_no], w_gate[section_no], w_up[section_no], w_down[section_no])
            section_inputs.append(grad_in)
            section_routes.append(grad_route)
        inputs.append(jnp.stack(section_inputs))
        routes.append(jnp.stack(section_routes))
    input_grad = jnp.stack(inputs)
    route_grad = jnp.stack(routes)
    prev_grad = jnp.concatenate([input_grad[1:], jnp.zeros_like(input_grad[:1])], axis=0)
    return prev_grad, route_grad
```

```python
import functools

import jax
import jax.numpy as jnp
from jax import lax
from jax.experimental import pallas as pl
from jax.experimental.pallas import tpu as pltpu
from jax.sharding import PartitionSpec as P

MESH = pl.DeviceIdType.MESH
F32 = jnp.float32
BF16 = jnp.bfloat16
NT = (((1,), (1,)), ((), ()))
TN = (((0,), (0,)), ((), ()))
window_expert = 0


def split(total, most):
    best = 128
    for width in range(128, most + 1, 128):
        if total % width == 0:
            best = width
    return best


def kernel(
    sections, n, cfg,
    dy_hbm, ids_hbm, wt_hbm, gate_hbm, up_hbm, wg_hbm, wu_hbm, wd_hbm,
    lrecv, early_r, pick_r, route_out,
    dy_v, ids_v, wt_v, gate_v, up_v, wg_v, wu_v, wd_v,
    rows_v, late_v, early_v, pick_v, wcol_v,
    a_v, b_v, q_v, dg_v, du_v, racc_v, rsend_v, rrecv_v,
    psend, precv, keep, ysend, yrecv, lsend,
    in_sem, wd_sem, wg_sem, wu_sem,
    gy_send, gy_recv, gp_send, gp_recv, rl_send, rl_recv,
    p_send, p_recv, y_send, y_recv, l_send, l_recv,
    e_send, e_recv, k_send, k_recv, r_send, r_recv,
):
    micro, tok, cap, wd_w, nd, wc, nc, fw, nf = cfg
    chips = n // 2
    blk = micro * cap
    rows = n * blk
    spare = tok - cap
    sec = lax.axis_index("section")
    me = lax.axis_index("fsdp")
    core = lax.rem(me, 2)
    chip = me // 2
    partner = chip * 2 + (1 - core)
    has_prev = sec > 0
    has_next = sec < sections - 1

    def local(src, dst, sem):
        return pltpu.make_async_copy(src, dst, sem)

    def remote(src, dst, ssem, rsem, to):
        return pltpu.make_async_remote_copy(
            src_ref=src, dst_ref=dst, send_sem=ssem, recv_sem=rsem,
            device_id=to, device_id_type=MESH,
        )

    barrier = pltpu.get_barrier_semaphore()
    for k in range(1, n):
        pl.semaphore_signal(
            barrier, inc=1, device_id={"fsdp": lax.rem(me + k, n)}, device_id_type=MESH
        )

    @pl.when(has_prev)
    def _():
        pl.semaphore_signal(barrier, inc=1, device_id={"section": sec - 1}, device_id_type=MESH)

    @pl.when(has_next)
    def _():
        pl.semaphore_signal(barrier, inc=1, device_id={"section": sec + 1}, device_id_type=MESH)

    c_ids = local(ids_hbm, ids_v, in_sem.at[0])
    c_wt = local(wt_hbm, wt_v, in_sem.at[1])
    c_dy = local(dy_hbm, dy_v, in_sem.at[2])
    c_ids.start()
    c_wt.start()
    c_dy.start()
    c_gate = [local(gate_hbm.at[m], gate_v.at[:, m], in_sem.at[3 + m]) for m in range(micro)]
    c_up = [local(up_hbm.at[m], up_v.at[:, m], in_sem.at[3 + micro + m]) for m in range(micro)]
    for m in range(micro):
        c_gate[m].start()
        c_up[m].start()

    def wd_copy(d):
        return local(
            wd_hbm.at[:, pl.ds(pl.multiple_of(d * wd_w, wd_w), wd_w)], wd_v.at[d], wd_sem.at[d]
        )

    def wg_copy(c):
        return local(wg_hbm.at[pl.ds(pl.multiple_of(c * wc, wc), wc)], wg_v.at[c], wg_sem.at[c])

    def wu_copy(c):
        return local(wu_hbm.at[pl.ds(pl.multiple_of(c * wc, wc), wc)], wu_v.at[c], wu_sem.at[c])

    c_ids.wait()
    c_wt.wait()
    t_row = lax.broadcasted_iota(jnp.int32, (tok, tok), 0)
    t_col = lax.broadcasted_iota(jnp.int32, (tok, tok), 1)
    before = (t_row < t_col).astype(BF16)
    every = jnp.ones((tok, tok), BF16)
    lane = lax.broadcasted_iota(jnp.int32, (1, tok), 1).astype(F32)
    takes = []
    picks = []
    for m in range(micro):
        names = ids_v[m]
        routed = jnp.max((names == window_expert).astype(F32), axis=0, keepdims=True)
        r8 = jnp.broadcast_to(routed, (8, tok)).astype(BF16)
        order = jnp.dot(r8, before, preferred_element_type=F32)[0:1]
        count = jnp.dot(r8, every, preferred_element_type=F32)[0:1]
        free = lane - order
        slot = jnp.where(
            routed > 0.5, order, jnp.where(free < spare, cap + free, count + free - spare)
        )
        pick = (slot == t_row.astype(F32)).astype(F32)
        take = pick[:cap] * routed
        w_row = wt_v[m : m + 1, :].astype(F32)
        wcol_v[m * cap : (m + 1) * cap, :] = jnp.broadcast_to(
            jnp.sum(take * w_row, axis=1, keepdims=True), (cap, 128)
        )
        pick_v[m] = pick.astype(BF16)
        takes.append(take)
        picks.append(pick.astype(BF16))
    c_dy.wait()
    for d in range(nd):
        wd_copy(d).start()
    for c in range(nc):
        wg_copy(c).start()
        wu_copy(c).start()
    for d in range(nd):
        cols = slice(d * wd_w, (d + 1) * wd_w)
        for m in range(micro):
            rows_v[d, me, m * cap : (m + 1) * cap, :] = jnp.dot(
                takes[m].astype(BF16), dy_v[m, :, cols], preferred_element_type=F32
            ).astype(BF16)
        if d == 0:
            pl.semaphore_wait(
                barrier, n - 1 + has_prev.astype(jnp.int32) + has_next.astype(jnp.int32)
            )

        for k in range(1, chips):
            other = lax.rem(chip + k, chips)
            remote(
                rows_v.at[d, me], rows_v.at[d, me], gy_send.at[d, k], gy_recv.at[d, chip],
                {"fsdp": other * 2 + core},
            ).start()
        remote(
            rows_v.at[d, me], rows_v.at[d, me], gp_send.at[d], gp_recv.at[d], {"fsdp": partner}
        ).start()

    def early_copy():
        return remote(early_v, early_r, e_send, e_recv, {"section": sec - 1})

    def pick_copy():
        return remote(pick_v, pick_r, k_send, k_recv, {"section": sec - 1})

    for m in range(micro):
        for c in range(nc):
            cols = slice(c * wc, (c + 1) * wc)
            mix = jnp.dot(picks[m], dy_v[m, :, cols], preferred_element_type=F32)
            late_v[c, m * cap : (m + 1) * cap, :] = mix[:cap].astype(BF16)
            early_v[c, m * spare : (m + 1) * spare, :] = mix[cap:].astype(BF16)

    @pl.when(has_prev)
    def _():
        pick_copy().start()
        early_copy().start()

    for m in range(micro):
        c_gate[m].wait()
        c_up[m].wait()
    step = 32

    def terms(i, carry):
        at = i // micro
        m = lax.rem(i, micro)
        g = gate_v[at, m].astype(F32)
        u = up_v[at, m].astype(F32)
        sg = 1.0 / (1.0 + jnp.exp(-g))
        a_v[i] = u * sg * (1.0 + g * (1.0 - sg))
        b_v[i] = g * sg
        return carry

    lax.fori_loop(0, n * micro, terms, 0)

    def relay(d):
        for k in range(1, chips):
            other = lax.rem(chip + k, chips)
            at = other * 2 + core
            remote(
                rows_v.at[d, at], rows_v.at[d, at], gy_send.at[d, k], gy_recv.at[d, other],
                {"fsdp": at},
            ).wait_recv()
            remote(
                rows_v.at[d, at], rows_v.at[d, at], rl_send.at[d, k], rl_recv.at[d, other],
                {"fsdp": partner},
            ).start()

    def relayed(d):
        remote(
            rows_v.at[d, partner], rows_v.at[d, partner], gp_send.at[d], gp_recv.at[d],
            {"fsdp": partner},
        ).wait_recv()
        for k in range(1, chips):
            other = lax.rem(chip + k, chips)
            at = other * 2 + (1 - core)
            remote(
                rows_v.at[d, at], rows_v.at[d, at], rl_send.at[d, k], rl_recv.at[d, other],
                {"fsdp": partner},
            ).wait_recv()

    relay(0)
    for d in range(nd):
        if d + 1 < nd:
            relay(d + 1)
            wd_copy(d).wait()
            relayed(d)
            x = rows_v[d].reshape(rows, wd_w)
            for f in range(nf):
                part = lax.dot_general(
                    x, wd_v[d, f * fw : (f + 1) * fw, :], NT, preferred_element_type=F32
                )
                if d == 0:
                    q_v[f] = part
                else:
                    q_v[f] += part
        else:
            wd_copy(d).wait()
            relayed(d)
            x = rows_v[d].reshape(rows, wd_w)
            route = jnp.zeros((rows, 1), F32)
            for f in range(nf):
                cols = slice(f * fw, (f + 1) * fw)
                q = lax.dot_general(x, wd_v[d, cols, :], NT, preferred_element_type=F32)
                if nd > 1:
                    q = q + q_v[f]
                d_up = q * b_v[:, :, cols].reshape(rows, fw)
                u = up_v[:, :, :, cols].reshape(rows, fw).astype(F32)
                dg_v[:, cols] = (q * a_v[:, :, cols].reshape(rows, fw)).astype(BF16)
                du_v[:, cols] = d_up.astype(BF16)
                route = route + jnp.sum(d_up * u, axis=1, keepdims=True)
            racc_v[...] = jnp.broadcast_to(route, (rows, 128)).reshape(n, blk, 128)

    eye = (
        lax.broadcasted_iota(jnp.int32, (blk, 128), 0)
        == lax.broadcasted_iota(jnp.int32, (blk, 128), 1)
    ).astype(F32)
    for k in range(n):
        to = lax.rem(me + k, n)
        row = jnp.sum(racc_v[to] * eye, axis=0, keepdims=True)
        rsend_v[k] = jnp.broadcast_to(row, (8, 128))

    def route_copy(k):
        return remote(
            rsend_v.at[k], rrecv_v.at[k], r_send.at[k], r_recv.at[k],
            {"fsdp": lax.rem(me + k, n)},
        )

    def pair_copy(c):
        return remote(psend.at[c], precv.at[c], p_send.at[c], p_recv.at[c], {"fsdp": partner})

    def y_copy(c, k):
        return remote(
            ysend.at[c, k], yrecv.at[c, k], y_send.at[c, k], y_recv.at[c, k],
            {"fsdp": lax.rem(chip + k, chips) * 2 + core},
        )

    def late_copy(c):
        return remote(lsend.at[c], lrecv.at[c], l_send.at[c], l_recv.at[c], {"section": sec - 1})

    def compute(c):
        wg_copy(c).wait()
        wu_copy(c).wait()
        back = lax.dot_general(dg_v[...], wg_v[c], NT, preferred_element_type=F32)
        back = back + lax.dot_general(du_v[...], wu_v[c], NT, preferred_element_type=F32)
        back = back.reshape(chips, 2, blk, wc)
        is0 = (core == 0).astype(F32)
        first, second = back[:, 0], back[:, 1]
        mine = jnp.where(is0 > 0.5, first, second)
        theirs = jnp.where(is0 > 0.5, second, first)
        psend[c] = theirs.astype(BF16)
        keep[c] = mine
        pair_copy(c).start()

    def chip_sum(c):
        pair_copy(c).wait_recv()
        for k in range(1, chips):
            at = lax.rem(chip + k, chips)
            ysend[c, k] = (keep[c, at] + precv[c, at].astype(F32)).astype(BF16)
            y_copy(c, k).start()

    def finish(c):
        total = keep[c, chip] + precv[c, chip].astype(F32)
        for k in range(1, chips):
            y_copy(c, k).wait_recv()
            total = total + yrecv[c, k].astype(F32)
        lsend[c] = (late_v[c].astype(F32) + wcol_v[:, 0:1] * total).astype(BF16)

        @pl.when(has_prev)
        def _():
            late_copy(c).start()

    lag_y = 5

    def body(i, carry):
        @pl.when(i < nc)
        def _():
            compute(i)

        @pl.when(jnp.logical_and(i >= 1, i - 1 < nc))
        def _():
            chip_sum(i - 1)

        @pl.when(i >= lag_y)
        def _():
            finish(i - lag_y)

        return carry

    for k in range(1, n):
        route_copy(k).start()
    lax.fori_loop(0, nc + lag_y, body, 0)

    total = rsend_v[0]
    for k in range(1, n):
        route_copy(k).wait_recv()
        total = total + rrecv_v[k]
    col = jnp.sum(eye * total[0:1], axis=1, keepdims=True)
    for m in range(micro):
        route_out[m : m + 1, :] = jnp.sum(
            takes[m] * col[m * cap : (m + 1) * cap], axis=0, keepdims=True
        )

    for d in range(nd):
        remote(
            rows_v.at[d, me], rows_v.at[d, me], gp_send.at[d], gp_recv.at[d], {"fsdp": partner}
        ).wait_send()
        for k in range(1, chips):
            at = lax.rem(chip + k, chips) * 2 + core
            remote(
                rows_v.at[d, me], rows_v.at[d, me], gy_send.at[d, k], gy_recv.at[d, chip],
                {"fsdp": at},
            ).wait_send()
            remote(
                rows_v.at[d, at], rows_v.at[d, at], rl_send.at[d, k], rl_recv.at[d, chip],
                {"fsdp": partner},
            ).wait_send()
    for k in range(1, n):
        route_copy(k).wait_send()

    def drain(c, carry):
        pair_copy(c).wait_send()
        for k in range(1, chips):
            y_copy(c, k).wait_send()

        @pl.when(has_prev)
        def _():
            late_copy(c).wait_send()

        @pl.when(has_next)
        def _():
            late_copy(c).wait_recv()

        return carry

    lax.fori_loop(0, nc, drain, 0)

    @pl.when(has_prev)
    def _():
        pick_copy().wait_send()
        early_copy().wait_send()

    @pl.when(has_next)
    def _():
        pick_copy().wait_recv()
        early_copy().wait_recv()


def place(sections, nc, wc, late, early, pick, route, out, route_out):
    keep = lax.axis_index("section") < sections - 1
    for c in range(nc):
        mixed = jnp.concatenate([late[c], early[c]], axis=0)
        mixed = lax.dot_general(pick[0], mixed, TN, preferred_element_type=F32)
        out[0, :, c * wc : (c + 1) * wc] = jnp.where(keep, mixed, 0.0).astype(BF16)
    route_out[...] = route[...]


def solution(mesh):
    sections = mesh.shape["section"]
    n = mesh.shape["fsdp"]

    def local(out_grad, expert_ids, route_weight, gate_pre, up_pre, w_gate, w_up, w_down):
        micro, tok, width = out_grad.shape[1:]
        cap = gate_pre.shape[2] // n
        ff = gate_pre.shape[3]
        chips = n // 2
        blk = micro * cap
        rows = n * blk
        spare = tok - cap
        wd_w = split(width, 512)
        wc = split(width, 256)
        fw = split(ff, 512)
        nd, nc, nf = width // wd_w, width // wc, ff // fw
        cfg = (micro, tok, cap, wd_w, nd, wc, nc, fw, nf)
        any_spec = pl.BlockSpec(memory_space=pl.ANY)
        vm = pltpu.VMEM
        dma = pltpu.SemaphoreType.DMA
        late, early, pick, route = pl.pallas_call(
            functools.partial(kernel, sections, n, cfg),
            out_shape=(
                jax.ShapeDtypeStruct((nc, blk, wc), BF16),
                jax.ShapeDtypeStruct((nc, micro * spare, wc), BF16),
                jax.ShapeDtypeStruct((micro, tok, tok), BF16),
                jax.ShapeDtypeStruct((micro, tok), F32),
            ),
            in_specs=[any_spec] * 8,
            out_specs=(any_spec, any_spec, any_spec, pl.BlockSpec(memory_space=pltpu.VMEM)),
            scratch_shapes=[
                vm((micro, tok, width), BF16),
                vm((micro, expert_ids.shape[3], tok), jnp.int32),
                vm((micro, tok), BF16),
                vm((n, micro, cap, ff), BF16),
                vm((n, micro, cap, ff), BF16),
                vm((nc, wc, ff), BF16),
                vm((nc, wc, ff), BF16),
                vm((nd, ff, wd_w), BF16),
                vm((nd, n, blk, wd_w), BF16),
                vm((nc, blk, wc), BF16),
                vm((nc, micro * spare, wc), BF16),
                vm((micro, tok, tok), BF16),
                vm((blk, 128), F32),
                vm((n * micro, cap, ff), F32),
                vm((n * micro, cap, ff), F32),
                vm((nf, rows, fw), F32),
                vm((rows, ff), BF16),
                vm((rows, ff), BF16),
                vm((n, blk, 128), F32),
                vm((n, 8, 128), F32),
                vm((n, 8, 128), F32),
                vm((nc, chips, blk, wc), BF16),
                vm((nc, chips, blk, wc), BF16),
                vm((nc, chips, blk, wc), F32),
                vm((nc, chips, blk, wc), BF16),
                vm((nc, chips, blk, wc), BF16),
                vm((nc, blk, wc), BF16),
                dma((3 + 2 * micro,)),
                dma((nd,)), dma((nc,)), dma((nc,)),
                dma((nd, chips)), dma((nd, chips)),
                dma((nd,)), dma((nd,)),
                dma((nd, chips)), dma((nd, chips)),
                dma((nc,)), dma((nc,)),
                dma((nc, chips)), dma((nc, chips)),
                dma((nc,)), dma((nc,)),
                dma, dma, dma, dma,
                dma((n,)), dma((n,)),
            ],
            compiler_params=pltpu.CompilerParams(
                collective_id=0, has_side_effects=True, vmem_limit_bytes=67043328
            ),
        )(
            out_grad[0],
            jnp.swapaxes(expert_ids[0], 1, 2),
            route_weight[0],
            gate_pre[0].reshape(micro, n, cap, ff),
            up_pre[0].reshape(micro, n, cap, ff),
            w_gate[0],
            w_up[0],
            w_down[0],
        )
        prev, route = pl.pallas_call(
            functools.partial(place, sections, nc, wc),
            grid=(micro,),
            out_shape=(
                jax.ShapeDtypeStruct((micro, tok, width), BF16),
                jax.ShapeDtypeStruct((micro, tok), F32),
            ),
            in_specs=[
                pl.BlockSpec((nc, cap, wc), lambda m: (0, m, 0)),
                pl.BlockSpec((nc, spare, wc), lambda m: (0, m, 0)),
                pl.BlockSpec((1, tok, tok), lambda m: (m, 0, 0)),
                pl.BlockSpec((micro, tok), lambda m: (0, 0)),
            ],
            out_specs=(
                pl.BlockSpec((1, tok, width), lambda m: (m, 0, 0)),
                pl.BlockSpec((micro, tok), lambda m: (0, 0)),
            ),
        )(
            late,
            early,
            pick,
            route,
        )
        return prev[None], route[None]

    return jax.shard_map(
        local,
        mesh=mesh,
        in_specs=(
            P("section", None, "fsdp", None),
            P("section", None, "fsdp", None),
            P("section", None, "fsdp"),
            P("section", None, None, "fsdp"),
            P("section", None, None, "fsdp"),
            P("section", None, "fsdp"),
            P("section", None, "fsdp"),
            P("section", "fsdp", None),
        ),
        out_specs=(P("section", None, "fsdp", None), P("section", None, "fsdp")),
        check_vma=False,
    )
```

```python
import functools

import jax
import jax.numpy as jnp
from jax import lax
from jax.experimental import pallas as pl
from jax.experimental.pallas import tpu as pltpu
from jax.sharding import PartitionSpec as P

MESH = pl.DeviceIdType.MESH
F32 = jnp.float32
BF16 = jnp.bfloat16
NT = (((1,), (1,)), ((), ()))
TN = (((0,), (0,)), ((), ()))
window_expert = 0


def split(total, most):
    best = 128
    for width in range(128, most + 1, 128):
        if total % width == 0:
            best = width
    return best


def spans(units):
    size = 2 if units % 2 == 0 else 1
    return [(at, size) for at in range(0, units, size)]


def kernel(
    sections, n, cfg,
    dy_hbm, ids_hbm, wt_hbm, gate_hbm, up_hbm, wg_hbm, wu_hbm, wd_hbm,
    lrecv, early_r, pick_r, route_out,
    dy_v, ids_v, wt_v, gate_v, up_v, wg_v, wu_v, wd_v,
    rows_v, late_v, early_v, pick_v, wcol_v,
    a_v, b_v, q_v, dg_v, du_v, racc_v, rsend_v, rrecv_v, route_v,
    psend, precv, keep, ysend, yrecv, lsend,
    in_sem, g_sem, u_sem, wd_sem, wg_sem, wu_sem,
    gy_send, gy_recv, gp_send, gp_recv, rl_send, rl_recv,
    p_send, p_recv, y_send, y_recv, l_send, l_recv,
    e_send, e_recv, k_send, k_recv, r_send, r_recv,
):
    micro, tok, cap, wd_w, nd, wc, nc, fw, nf = cfg
    chips = n // 2
    blk = micro * cap
    rows = n * blk
    half = chips * blk
    spare = tok - cap
    parts = spans(nc)
    steps = len(parts)
    size = parts[0][1]
    per = size
    last = steps - 1
    sec = lax.axis_index("section")
    me = lax.axis_index("fsdp")
    core = lax.rem(me, 2)
    chip = me // 2
    partner = chip * 2 + (1 - core)
    has_prev = sec > 0
    has_next = sec < sections - 1

    def local(src, dst, sem):
        return pltpu.make_async_copy(src, dst, sem)

    def remote(src, dst, ssem, rsem, to):
        return pltpu.make_async_remote_copy(
            src_ref=src, dst_ref=dst, send_sem=ssem, recv_sem=rsem,
            device_id=to, device_id_type=MESH,
        )

    c_ids = local(ids_hbm, ids_v, in_sem.at[0])
    c_wt = local(wt_hbm, wt_v, in_sem.at[1])
    c_dy = local(dy_hbm, dy_v, in_sem.at[2])
    c_ids.start()
    c_dy.start()
    c_wt.start()

    barrier = pltpu.get_barrier_semaphore()
    for k in range(1, n):
        pl.semaphore_signal(
            barrier, inc=1, device_id={"fsdp": lax.rem(me + k, n)}, device_id_type=MESH
        )

    @pl.when(has_prev)
    def _():
        pl.semaphore_signal(barrier, inc=1, device_id={"section": sec - 1}, device_id_type=MESH)

    @pl.when(has_next)
    def _():
        pl.semaphore_signal(barrier, inc=1, device_id={"section": sec + 1}, device_id_type=MESH)

    c_gate = []
    c_up = []
    for m in range(micro):
        for r in range(2):
            side = core if r == 0 else 1 - core
            at = m * 2 + r
            c_gate.append(local(gate_hbm.at[m, :, side], gate_v.at[r, :, m], g_sem.at[at]))
            c_up.append(local(up_hbm.at[m, :, side], up_v.at[r, :, m], u_sem.at[at]))

    def wd_copy(d):
        return local(wd_hbm.at[:, d * wd_w : (d + 1) * wd_w], wd_v.at[d], wd_sem.at[d])

    def unit(i):
        return pl.ds(i * size, size)

    def wg_copy(i):
        return local(wg_hbm.at[unit(i)], wg_v.at[unit(i)], wg_sem.at[i])

    def wu_copy(i):
        return local(wu_hbm.at[unit(i)], wu_v.at[unit(i)], wu_sem.at[i])

    t_row = lax.broadcasted_iota(jnp.int32, (tok, tok), 0)
    t_col = lax.broadcasted_iota(jnp.int32, (tok, tok), 1)
    before = (t_row < t_col).astype(BF16)
    every = jnp.ones((tok, tok), BF16)
    lane = lax.broadcasted_iota(jnp.int32, (1, tok), 1).astype(F32)
    row_f = t_row.astype(F32)
    c_ids.wait()
    routeds, orders, counts, takes = [], [], [], []
    for m in range(micro):
        routed = jnp.max((ids_v[m] == window_expert).astype(F32), axis=0, keepdims=True)
        r8 = jnp.broadcast_to(routed, (8, tok)).astype(BF16)
        order = jnp.dot(r8, before, preferred_element_type=F32)[0:1]
        routeds.append(routed)
        orders.append(order)
        takes.append(jnp.where(row_f[:cap] == order, routed, 0.0))
    takes_b = [take.astype(BF16) for take in takes]
    c_dy.wait()

    def send_rows(d):
        for k in range(1, chips):
            other = lax.rem(chip + k, chips)
            remote(
                rows_v.at[d, 0, chip], rows_v.at[d, 0, chip], gy_send.at[d, k], gy_recv.at[d, chip],
                {"fsdp": other * 2 + core},
            ).start()
        remote(
            rows_v.at[d, 0, chip], rows_v.at[d, 1, chip], gp_send.at[d], gp_recv.at[d],
            {"fsdp": partner},
        ).start()

    for d in range(nd):
        cols = slice(d * wd_w, (d + 1) * wd_w)
        for m in range(micro):
            rows_v[d, 0, chip, m * cap : (m + 1) * cap, :] = jnp.dot(
                takes_b[m], dy_v[m, :, cols], preferred_element_type=F32
            ).astype(BF16)
        if d == 0:
            wd_copy(0).start()
            pl.semaphore_wait(
                barrier, n - 1 + has_prev.astype(jnp.int32) + has_next.astype(jnp.int32)
            )
        send_rows(d)
        if d == 0:
            for copy in c_gate + c_up:
                copy.start()
        if d > 0:
            wd_copy(d).start()
    for i in range(len(parts)):
        wg_copy(i).start()
        wu_copy(i).start()

    def early_copy():
        return remote(early_v, early_r, e_send, e_recv, {"section": sec - 1})

    def pick_copy():
        return remote(pick_v, pick_r, k_send, k_recv, {"section": sec - 1})

    c_wt.wait()
    picks = []
    for m in range(micro):
        routed, order = routeds[m], orders[m]
        r8 = jnp.broadcast_to(routed, (8, tok)).astype(BF16)
        count = jnp.dot(r8, every, preferred_element_type=F32)[0:1]
        free = lane - order
        slot = jnp.where(
            routed > 0.5, order, jnp.where(free < spare, cap + free, count + free - spare)
        )
        pick = (slot == row_f).astype(BF16)
        w_row = wt_v[m : m + 1, :].astype(F32)
        wcol_v[m * cap : (m + 1) * cap, :] = jnp.broadcast_to(
            jnp.sum(takes[m] * w_row, axis=1, keepdims=True), (cap, 128)
        )
        pick_v[m] = pick
        picks.append(pick)
    for m in range(micro):
        for d in range(nd):
            cols = slice(d * wd_w, (d + 1) * wd_w)
            mix = jnp.dot(picks[m], dy_v[m, :, cols], preferred_element_type=F32)
            for j in range(wd_w // wc):
                late_v[d * (wd_w // wc) + j, m * cap : (m + 1) * cap, :] = mix[:cap, j * wc : (j + 1) * wc].astype(BF16)
            early_v[m * spare : (m + 1) * spare, cols] = mix[cap:].astype(BF16)

    @pl.when(has_prev)
    def _():
        pick_copy().start()
        early_copy().start()

    for copy in c_gate + c_up:
        copy.wait()

    def terms(i, carry):
        r = i // (chips * micro)
        j = lax.rem(i, chips * micro)
        at = j // micro
        m = lax.rem(j, micro)
        g = gate_v[r, at, m].astype(F32)
        u = up_v[r, at, m].astype(F32)
        sg = 1.0 / (1.0 + jnp.exp(-g))
        a_v[i] = u * sg * (1.0 + g * (1.0 - sg))
        b_v[i] = g * sg
        return carry

    lax.fori_loop(0, n * micro, terms, 0)

    def relay(d):
        for k in range(1, chips):
            other = lax.rem(chip + k, chips)
            remote(
                rows_v.at[d, 0, other], rows_v.at[d, 0, other], gy_send.at[d, k],
                gy_recv.at[d, other], {"fsdp": other * 2 + core},
            ).wait_recv()
            remote(
                rows_v.at[d, 0, other], rows_v.at[d, 1, other], rl_send.at[d, k],
                rl_recv.at[d, other], {"fsdp": partner},
            ).start()

    def relayed(d):
        remote(
            rows_v.at[d, 0, chip], rows_v.at[d, 1, chip], gp_send.at[d], gp_recv.at[d],
            {"fsdp": partner},
        ).wait_recv()
        for k in range(1, chips):
            other = lax.rem(chip + k, chips)
            remote(
                rows_v.at[d, 0, other], rows_v.at[d, 1, other], rl_send.at[d, k],
                rl_recv.at[d, other], {"fsdp": partner},
            ).wait_recv()

    def sent_rows():
        for d in range(nd):
            remote(
                rows_v.at[d, 0, chip], rows_v.at[d, 1, chip], gp_send.at[d], gp_recv.at[d],
                {"fsdp": partner},
            ).wait_send()
            for k in range(1, chips):
                other = lax.rem(chip + k, chips)
                remote(
                    rows_v.at[d, 0, chip], rows_v.at[d, 0, chip], gy_send.at[d, k],
                    gy_recv.at[d, chip], {"fsdp": other * 2 + core},
                ).wait_send()
                remote(
                    rows_v.at[d, 0, other], rows_v.at[d, 1, other], rl_send.at[d, k],
                    rl_recv.at[d, other], {"fsdp": partner},
                ).wait_send()

    def sent_early():
        @pl.when(has_prev)
        def _():
            pick_copy().wait_send()
            early_copy().wait_send()

        @pl.when(has_next)
        def _():
            pick_copy().wait_recv()
            early_copy().wait_recv()

    relay(0)
    for d in range(nd):
        if d + 1 < nd:
            relay(d + 1)
        wd_copy(d).wait()
        relayed(d)
        x = rows_v[d].reshape(rows, wd_w)
        if d + 1 < nd:
            for f in range(nf):
                part = lax.dot_general(
                    x, wd_v[d, f * fw : (f + 1) * fw, :], NT, preferred_element_type=F32
                )
                if d == 0:
                    q_v[f] = part
                else:
                    q_v[f] += part
        else:
            route = jnp.zeros((rows, 128), F32)
            for f in range(nf):
                cols = slice(f * fw, (f + 1) * fw)
                q = lax.dot_general(x, wd_v[d, cols, :], NT, preferred_element_type=F32)
                if nd > 1:
                    q = q + q_v[f]
                d_up = q * b_v[:, :, cols].reshape(rows, fw)
                u = up_v[:, :, :, :, cols].reshape(rows, fw).astype(F32)
                dg_v[:, cols] = (q * a_v[:, :, cols].reshape(rows, fw)).astype(BF16)
                du_v[:, cols] = d_up.astype(BF16)
                term = d_up * u
                for j in range(fw // 128):
                    route = route + term[:, j * 128 : (j + 1) * 128]
            racc_v[...] = route

    eye = (
        lax.broadcasted_iota(jnp.int32, (blk, 128), 0)
        == lax.broadcasted_iota(jnp.int32, (blk, 128), 1)
    ).astype(F32)

    def route_copy(k):
        return remote(
            rsend_v.at[k], rrecv_v.at[k], r_send.at[k], r_recv.at[k],
            {"fsdp": lax.rem(me + k, n)},
        )

    def start_route():
        sums = jnp.sum(racc_v[...], axis=1, keepdims=True)
        racc_v[...] = jnp.broadcast_to(sums, (rows, 128))
        for k in range(n):
            to = lax.rem(me + k, n)
            side = lax.rem(to + core, 2)
            first = pl.multiple_of((side * chips + to // 2) * blk, blk)
            row = jnp.sum(racc_v[pl.ds(first, blk)] * eye, axis=0, keepdims=True)
            rsend_v[k] = jnp.broadcast_to(row, (8, 128))
        for k in range(1, n):
            route_copy(k).start()

    def end_route():
        total = rsend_v[0]
        for k in range(1, n):
            route_copy(k).wait_recv()
            total = total + rrecv_v[k]
        col = jnp.sum(eye * total[0:1], axis=1, keepdims=True)
        for m in range(micro):
            route_v[m : m + 1, :] = jnp.sum(
                takes[m] * col[m * cap : (m + 1) * cap], axis=0, keepdims=True
            )

    def route_store():
        return local(route_v, route_out, in_sem.at[3])

    def pair_copy(i):
        return remote(
            psend.at[unit(i)], precv.at[unit(i)], p_send.at[i], p_recv.at[i], {"fsdp": partner}
        )

    def y_copy(i, k, u=0, size=size):
        at = pl.ds(i * per + u, size)
        return remote(
            ysend.at[k - 1, at], yrecv.at[k - 1, at], y_send.at[i + u, k], y_recv.at[i + u, k],
            {"fsdp": lax.rem(chip + k, chips) * 2 + core},
        )

    def late_copy(i, u=0, size=size):
        at = pl.ds(i * per + u, size)
        return remote(
            lsend.at[at], lrecv.at[at], l_send.at[i + u], l_recv.at[i + u], {"section": sec - 1}
        )

    def compute(i):
        wg_copy(i).wait()
        wu_copy(i).wait()
        w = wg_v[unit(i)].reshape(size * wc, -1)
        back = lax.dot_general(dg_v[...], w, NT, preferred_element_type=F32)
        w = wu_v[unit(i)].reshape(size * wc, -1)
        back = back + lax.dot_general(du_v[...], w, NT, preferred_element_type=F32)
        for j in range(size):
            piece = back[:, j * wc : (j + 1) * wc]
            psend[i * size + j] = piece[half:].astype(BF16).reshape(chips, blk, wc)
            keep[i * size + j] = piece[:half].reshape(chips, blk, wc)
        pair_copy(i).start()

    def chip_sum(i, group=size):
        pair_copy(i).wait_recv()
        for u in range(0, size, group):
            for k in range(1, chips):
                other = lax.rem(chip + k, chips)
                for j in range(u, u + group):
                    at = i * size + j
                    ysend[k - 1, at] = (keep[at, other] + precv[at, other].astype(F32)).astype(BF16)
                y_copy(i, k, u, group).start()

    def finish(i, group=size):
        for u in range(0, size, group):
            for k in range(1, chips):
                y_copy(i, k, u, group).wait_recv()
            for j in range(u, u + group):
                at = i * size + j
                total = keep[at, chip] + precv[at, chip].astype(F32)
                for k in range(1, chips):
                    total = total + yrecv[k - 1, at].astype(F32)
                lsend[at] = (late_v[at].astype(F32) + wcol_v[:, 0:1] * total).astype(BF16)

            @pl.when(has_prev)
            def _():
                late_copy(i, u, group).start()

    def drain(i, group=size):
        pair_copy(i).wait_send()
        for u in range(0, size, group):
            for k in range(1, chips):
                y_copy(i, k, u, group).wait_send()

    def landed(i, group=size):
        for u in range(0, size, group):
            @pl.when(has_prev)
            def _():
                late_copy(i, u, group).wait_send()

            @pl.when(has_next)
            def _():
                late_copy(i, u, group).wait_recv()

    lag = 3

    def body(i, carry):
        compute(i)

        @pl.when(i >= 1)
        def _():
            chip_sum(i - 1)

        @pl.when(i == 2)
        def _():
            start_route()

        @pl.when(i >= lag)
        def _():
            finish(i - lag)

        return carry

    lax.fori_loop(0, steps, body, 0)
    if steps < 3:
        start_route()
    chip_sum(last, 1)
    for i in range(max(0, steps - lag), last):
        finish(i)
    end_route()
    route_store().start()
    sent_rows()
    for k in range(1, n):
        route_copy(k).wait_send()
    for i in range(last):
        drain(i)
    sent_early()
    finish(last, 1)
    drain(last, 1)
    route_store().wait()
    for i in range(last):
        landed(i)
    landed(last, 1)


def place(sections, cfg, late_v, early_v, pick_v, route_v, out_hbm, route_out, out_v, o_sem, s_sem):
    micro, tok, cap, pw, npw, wc = cfg
    per = pw // wc
    spare = tok - cap
    keep = lax.axis_index("section") < sections - 1
    c_route = pltpu.make_async_copy(route_v, route_out, s_sem)
    c_route.start()

    def store(c):
        cols = slice(c * pw, (c + 1) * pw)
        return pltpu.make_async_copy(out_v.at[:, :, cols], out_hbm.at[:, :, cols], o_sem.at[c])

    for c in range(npw):
        for m in range(micro):
            for j in range(c * per, (c + 1) * per):
                cols = slice(j * wc, (j + 1) * wc)
                mixed = jnp.concatenate(
                    [late_v[j, m * cap : (m + 1) * cap], early_v[m * spare : (m + 1) * spare, cols]],
                    axis=0,
                )
                mixed = lax.dot_general(pick_v[m], mixed, TN, preferred_element_type=F32)
                out_v[m, :, cols] = jnp.where(keep, mixed, 0.0).astype(BF16)
        store(c).start()
    for c in range(npw):
        store(c).wait()
    c_route.wait()


def solution(mesh):
    sections = mesh.shape["section"]
    n = mesh.shape["fsdp"]

    def local(out_grad, expert_ids, route_weight, gate_pre, up_pre, w_gate, w_up, w_down):
        micro, tok, width = out_grad.shape[1:]
        cap = gate_pre.shape[2] // n
        ff = gate_pre.shape[3]
        chips = n // 2
        blk = micro * cap
        rows = n * blk
        spare = tok - cap
        wd_w = split(width, 512)
        wc = split(width, 256)
        fw = split(ff, 512)
        nd, nc, nf = width // wd_w, width // wc, ff // fw
        np_ = len(spans(nc))
        cfg = (micro, tok, cap, wd_w, nd, wc, nc, fw, nf)
        any_spec = pl.BlockSpec(memory_space=pl.ANY)
        vm = pltpu.VMEM
        dma = pltpu.SemaphoreType.DMA
        late, early, pick, route = pl.pallas_call(
            functools.partial(kernel, sections, n, cfg),
            out_shape=(
                vm((nc, blk, wc), BF16),
                vm((micro * spare, width), BF16),
                vm((micro, tok, tok), BF16),
                vm((micro, tok), F32),
            ),
            in_specs=[any_spec] * 8,
            out_specs=(any_spec,) * 4,
            scratch_shapes=[
                vm((micro, tok, width), BF16),
                vm((micro, expert_ids.shape[3], tok), jnp.int32),
                vm((micro, tok), BF16),
                vm((2, chips, micro, cap, ff), BF16),
                vm((2, chips, micro, cap, ff), BF16),
                vm((nc, wc, ff), BF16),
                vm((nc, wc, ff), BF16),
                vm((nd, ff, wd_w), BF16),
                vm((nd, 2, chips, blk, wd_w), BF16),
                vm((nc, blk, wc), BF16),
                vm((micro * spare, width), BF16),
                vm((micro, tok, tok), BF16),
                vm((blk, 128), F32),
                vm((n * micro, cap, ff), F32),
                vm((n * micro, cap, ff), F32),
                vm((nf, rows, fw), F32),
                vm((rows, ff), BF16),
                vm((rows, ff), BF16),
                vm((rows, 128), F32),
                vm((n, 8, 128), F32),
                vm((n, 8, 128), F32),
                vm((micro, tok), F32),
                vm((nc, chips, blk, wc), BF16),
                vm((nc, chips, blk, wc), BF16),
                vm((nc, chips, blk, wc), F32),
                vm((chips - 1, nc, blk, wc), BF16),
                vm((chips - 1, nc, blk, wc), BF16),
                vm((nc, blk, wc), BF16),
                dma((4,)),
                dma((2 * micro,)), dma((2 * micro,)),
                dma((nd,)), dma((np_,)), dma((np_,)),
                dma((nd, chips)), dma((nd, chips)),
                dma((nd,)), dma((nd,)),
                dma((nd, chips)), dma((nd, chips)),
                dma((np_,)), dma((np_,)),
                dma((np_ + 1, chips)), dma((np_ + 1, chips)),
                dma((np_ + 1,)), dma((np_ + 1,)),
                dma, dma, dma, dma,
                dma((n,)), dma((n,)),
            ],
            compiler_params=pltpu.CompilerParams(
                collective_id=0, has_side_effects=True, vmem_limit_bytes=62914560
            ),
        )(
            out_grad[0],
            jnp.swapaxes(expert_ids[0], 1, 2),
            route_weight[0],
            gate_pre[0].reshape(micro, chips, 2, cap, ff),
            up_pre[0].reshape(micro, chips, 2, cap, ff),
            w_gate[0].reshape(nc, wc, ff),
            w_up[0].reshape(nc, wc, ff),
            w_down[0],
        )
        late, early, pick, route = (
            pltpu.with_memory_space_constraint(x, pltpu.VMEM) for x in (late, early, pick, route)
        )
        pw = split(width, 1024)
        npw = width // pw
        prev, route = pl.pallas_call(
            functools.partial(place, sections, (micro, tok, cap, pw, npw, wc)),
            out_shape=(
                jax.ShapeDtypeStruct((micro, tok, width), BF16),
                jax.ShapeDtypeStruct((micro, tok), F32),
            ),
            in_specs=[pl.BlockSpec(memory_space=pltpu.VMEM)] * 4,
            out_specs=(any_spec, any_spec),
            scratch_shapes=[vm((micro, tok, width), BF16), dma((npw,)), dma],
        )(late, early, pick, route)
        return prev[None], route[None]

    return jax.shard_map(
        local,
        mesh=mesh,
        in_specs=(
            P("section", None, "fsdp", None),
            P("section", None, "fsdp", None),
            P("section", None, "fsdp"),
            P("section", None, None, "fsdp"),
            P("section", None, None, "fsdp"),
            P("section", None, "fsdp"),
            P("section", None, "fsdp"),
            P("section", "fsdp", None),
        ),
        out_specs=(P("section", None, "fsdp", None), P("section", None, "fsdp")),
        check_vma=False,
    )
```

```python
import functools

import jax
import jax.numpy as jnp
from jax import lax
from jax.experimental import pallas as pl
from jax.experimental.pallas import tpu as pltpu
from jax.sharding import PartitionSpec as P

MESH = pl.DeviceIdType.MESH
F32 = jnp.float32
BF16 = jnp.bfloat16
NT = (((1,), (1,)), ((), ()))
TN = (((0,), (0,)), ((), ()))
window_expert = 0
LASTW = 128
DIRECT = 1


def split(total, most):
    best = 128
    for width in range(128, most + 1, 128):
        if total % width == 0:
            best = width
    return best


def blocks(total, most):
    width = split(total, most)
    out = [(at, width) for at in range(0, total, width)]
    if LASTW and width > LASTW:
        at, _ = out.pop()
        out += [(at, width - LASTW), (at + width - LASTW, LASTW)]
    return out


def spans(units):
    size = 2 if units % 2 == 0 else 1
    return [(at, size) for at in range(0, units, size)]


def kernel(
    sections, n, cfg,
    dy_hbm, ids_hbm, wt_hbm, gate_hbm, up_hbm, wg_hbm, wu_hbm, wd_hbm,
    lrecv, early_r, pick_r, route_out,
    dy_v, ids_v, wt_v, gate_v, up_v, wg_v, wu_v, wd_v,
    rows_v, late_v, early_v, pick_v, wcol_v,
    a_v, b_v, q_v, dg_v, du_v, racc_v, rsend_v, rrecv_v, route_v,
    psend, precv, keep, ysend, yrecv, lsend,
    in_sem, g_sem, u_sem, wd_sem, wg_sem, wu_sem,
    gy_send, gy_recv, gp_send, gp_recv, rl_send, rl_recv,
    p_send, p_recv, y_send, y_recv, l_send, l_recv,
    e_send, e_recv, k_send, k_recv, r_send, r_recv,
):
    micro, tok, cap, cuts, wc, nc, fw, nf = cfg
    nd = len(cuts)
    chips = n // 2
    blk = micro * cap
    rows = n * blk
    half = chips * blk
    spare = tok - cap
    parts = spans(nc)
    steps = len(parts)
    size = parts[0][1]
    per = size
    last = steps - 1
    sec = lax.axis_index("section")
    me = lax.axis_index("fsdp")
    core = lax.rem(me, 2)
    chip = me // 2
    partner = chip * 2 + (1 - core)
    has_prev = sec > 0
    has_next = sec < sections - 1

    def local(src, dst, sem):
        return pltpu.make_async_copy(src, dst, sem)

    def remote(src, dst, ssem, rsem, to):
        return pltpu.make_async_remote_copy(
            src_ref=src, dst_ref=dst, send_sem=ssem, recv_sem=rsem,
            device_id=to, device_id_type=MESH,
        )

    c_ids = local(ids_hbm, ids_v, in_sem.at[0])
    c_wt = local(wt_hbm, wt_v, in_sem.at[1])
    c_dy = local(dy_hbm, dy_v, in_sem.at[2])
    c_ids.start()
    c_dy.start()
    c_wt.start()

    barrier = pltpu.get_barrier_semaphore()
    for k in range(1, n):
        pl.semaphore_signal(
            barrier, inc=1, device_id={"fsdp": lax.rem(me + k, n)}, device_id_type=MESH
        )

    @pl.when(has_prev)
    def _():
        pl.semaphore_signal(barrier, inc=1, device_id={"section": sec - 1}, device_id_type=MESH)

    @pl.when(has_next)
    def _():
        pl.semaphore_signal(barrier, inc=1, device_id={"section": sec + 1}, device_id_type=MESH)

    c_gate = []
    c_up = []
    for m in range(micro):
        for r in range(2):
            side = core if r == 0 else 1 - core
            at = m * 2 + r
            c_gate.append(local(gate_hbm.at[m, :, side], gate_v.at[r, :, m], g_sem.at[at]))
            c_up.append(local(up_hbm.at[m, :, side], up_v.at[r, :, m], u_sem.at[at]))

    def cut(d):
        at, size = cuts[d]
        return slice(at, at + size)

    def wd_copy(d):
        return local(wd_hbm.at[:, cut(d)], wd_v.at[:, cut(d)], wd_sem.at[d])

    def unit(i):
        return pl.ds(i * size, size)

    def wg_copy(i):
        return local(wg_hbm.at[unit(i)], wg_v.at[unit(i)], wg_sem.at[i])

    def wu_copy(i):
        return local(wu_hbm.at[unit(i)], wu_v.at[unit(i)], wu_sem.at[i])

    t_row = lax.broadcasted_iota(jnp.int32, (tok, tok), 0)
    t_col = lax.broadcasted_iota(jnp.int32, (tok, tok), 1)
    before = (t_row < t_col).astype(BF16)
    every = jnp.ones((tok, tok), BF16)
    lane = lax.broadcasted_iota(jnp.int32, (1, tok), 1).astype(F32)
    row_f = t_row.astype(F32)
    c_ids.wait()
    routeds, orders, counts, takes = [], [], [], []
    for m in range(micro):
        routed = jnp.max((ids_v[m] == window_expert).astype(F32), axis=0, keepdims=True)
        r8 = jnp.broadcast_to(routed, (8, tok)).astype(BF16)
        order = jnp.dot(r8, before, preferred_element_type=F32)[0:1]
        routeds.append(routed)
        orders.append(order)
        takes.append(jnp.where(row_f[:cap] == order, routed, 0.0))
    takes_b = [take.astype(BF16) for take in takes]
    c_dy.wait()

    def rows_at(r, c, d):
        return rows_v.at[r, c, :, cut(d)]

    def y_rows(d, k, owner):
        return remote(
            rows_at(0, owner, d), rows_at(0, owner, d), gy_send.at[d, k], gy_recv.at[d, owner],
            {"fsdp": lax.rem(chip + k, chips) * 2 + core},
        )

    def cross_rows(d, k):
        return remote(
            rows_at(0, chip, d), rows_at(1, chip, d), rl_send.at[d, k], rl_recv.at[d, chip],
            {"fsdp": lax.rem(chip + k, chips) * 2 + 1 - core},
        )

    def relay_rows(d, k):
        other = lax.rem(chip + k, chips)
        return remote(
            rows_at(0, other, d), rows_at(1, other, d), rl_send.at[d, k], rl_recv.at[d, other],
            {"fsdp": partner},
        )

    def pair_rows(d):
        return remote(
            rows_at(0, chip, d), rows_at(1, chip, d), gp_send.at[d], gp_recv.at[d],
            {"fsdp": partner},
        )

    def straight(d):
        return DIRECT and d == nd - 1

    def send_rows(d):
        for k in range(1, chips):
            y_rows(d, k, chip).start()
            if straight(d):
                cross_rows(d, k).start()
        pair_rows(d).start()

    for d in range(nd):
        cols = cut(d)
        for m in range(micro):
            rows_v[0, chip, m * cap : (m + 1) * cap, cols] = jnp.dot(
                takes_b[m], dy_v[m, :, cols], preferred_element_type=F32
            ).astype(BF16)
        if d == 0:
            wd_copy(0).start()
            pl.semaphore_wait(
                barrier, n - 1 + has_prev.astype(jnp.int32) + has_next.astype(jnp.int32)
            )
        send_rows(d)
        if d == 0:
            for copy in c_gate + c_up:
                copy.start()
        if d > 0:
            wd_copy(d).start()
    for i in range(len(parts)):
        wg_copy(i).start()
        wu_copy(i).start()

    def early_copy():
        return remote(early_v, early_r, e_send, e_recv, {"section": sec - 1})

    def pick_copy():
        return remote(pick_v, pick_r, k_send, k_recv, {"section": sec - 1})

    c_wt.wait()
    picks = []
    for m in range(micro):
        routed, order = routeds[m], orders[m]
        r8 = jnp.broadcast_to(routed, (8, tok)).astype(BF16)
        count = jnp.dot(r8, every, preferred_element_type=F32)[0:1]
        free = lane - order
        slot = jnp.where(
            routed > 0.5, order, jnp.where(free < spare, cap + free, count + free - spare)
        )
        pick = (slot == row_f).astype(BF16)
        w_row = wt_v[m : m + 1, :].astype(F32)
        wcol_v[m * cap : (m + 1) * cap, :] = jnp.broadcast_to(
            jnp.sum(takes[m] * w_row, axis=1, keepdims=True), (cap, 128)
        )
        pick_v[m] = pick
        picks.append(pick)
    for m in range(micro):
        for j in range(nc):
            cols = slice(j * wc, (j + 1) * wc)
            mix = jnp.dot(picks[m], dy_v[m, :, cols], preferred_element_type=F32)
            late_v[j, m * cap : (m + 1) * cap, :] = mix[:cap].astype(BF16)
            early_v[m * spare : (m + 1) * spare, cols] = mix[cap:].astype(BF16)

    @pl.when(has_prev)
    def _():
        pick_copy().start()
        early_copy().start()

    for copy in c_gate + c_up:
        copy.wait()

    def terms(i, carry):
        r = i // (chips * micro)
        j = lax.rem(i, chips * micro)
        at = j // micro
        m = lax.rem(j, micro)
        g = gate_v[r, at, m].astype(F32)
        u = up_v[r, at, m].astype(F32)
        sg = 1.0 / (1.0 + jnp.exp(-g))
        a_v[i] = u * sg * (1.0 + g * (1.0 - sg))
        b_v[i] = g * sg
        return carry

    lax.fori_loop(0, n * micro, terms, 0)

    def relay(d):
        for k in range(1, chips):
            y_rows(d, k, lax.rem(chip + k, chips)).wait_recv()
            if not straight(d):
                relay_rows(d, k).start()

    def relayed(d):
        pair_rows(d).wait_recv()
        for k in range(1, chips):
            relay_rows(d, k).wait_recv()

    def sent_rows():
        for d in range(nd):
            pair_rows(d).wait_send()
            for k in range(1, chips):
                y_rows(d, k, chip).wait_send()
                if straight(d):
                    cross_rows(d, k).wait_send()
                else:
                    relay_rows(d, k).wait_send()

    def sent_early():
        @pl.when(has_prev)
        def _():
            pick_copy().wait_send()
            early_copy().wait_send()

        @pl.when(has_next)
        def _():
            pick_copy().wait_recv()
            early_copy().wait_recv()

    relay(0)
    for d in range(nd):
        if d + 1 < nd:
            relay(d + 1)
        wd_copy(d).wait()
        relayed(d)
        x = rows_v[:, :, :, cut(d)].reshape(rows, cuts[d][1])
        if d + 1 < nd:
            for f in range(nf):
                part = lax.dot_general(
                    x, wd_v[f * fw : (f + 1) * fw, cut(d)], NT, preferred_element_type=F32
                )
                if d == 0:
                    q_v[f] = part
                else:
                    q_v[f] += part
        else:
            route = jnp.zeros((rows, 128), F32)
            for f in range(nf):
                cols = slice(f * fw, (f + 1) * fw)
                q = lax.dot_general(x, wd_v[cols, cut(d)], NT, preferred_element_type=F32)
                if nd > 1:
                    q = q + q_v[f]
                d_up = q * b_v[:, :, cols].reshape(rows, fw)
                u = up_v[:, :, :, :, cols].reshape(rows, fw).astype(F32)
                dg_v[:, cols] = (q * a_v[:, :, cols].reshape(rows, fw)).astype(BF16)
                du_v[:, cols] = d_up.astype(BF16)
                term = d_up * u
                for j in range(fw // 128):
                    route = route + term[:, j * 128 : (j + 1) * 128]
            racc_v[...] = route

    eye = (
        lax.broadcasted_iota(jnp.int32, (blk, 128), 0)
        == lax.broadcasted_iota(jnp.int32, (blk, 128), 1)
    ).astype(F32)

    def route_copy(k):
        return remote(
            rsend_v.at[k], rrecv_v.at[k], r_send.at[k], r_recv.at[k],
            {"fsdp": lax.rem(me + k, n)},
        )

    def start_route():
        sums = jnp.sum(racc_v[...], axis=1, keepdims=True)
        racc_v[...] = jnp.broadcast_to(sums, (rows, 128))
        for k in range(n):
            to = lax.rem(me + k, n)
            side = lax.rem(to + core, 2)
            first = pl.multiple_of((side * chips + to // 2) * blk, blk)
            row = jnp.sum(racc_v[pl.ds(first, blk)] * eye, axis=0, keepdims=True)
            rsend_v[k] = jnp.broadcast_to(row, (8, 128))
        for k in range(1, n):
            route_copy(k).start()

    def end_route():
        total = rsend_v[0]
        for k in range(1, n):
            route_copy(k).wait_recv()
            total = total + rrecv_v[k]
        col = jnp.sum(eye * total[0:1], axis=1, keepdims=True)
        for m in range(micro):
            route_v[m : m + 1, :] = jnp.sum(
                takes[m] * col[m * cap : (m + 1) * cap], axis=0, keepdims=True
            )

    def route_store():
        return local(route_v, route_out, in_sem.at[3])

    def pair_copy(i):
        return remote(
            psend.at[unit(i)], precv.at[unit(i)], p_send.at[i], p_recv.at[i], {"fsdp": partner}
        )

    def y_copy(i, k, u=0, size=size):
        at = pl.ds(i * per + u, size)
        return remote(
            ysend.at[k - 1, at], yrecv.at[k - 1, at], y_send.at[i + u, k], y_recv.at[i + u, k],
            {"fsdp": lax.rem(chip + k, chips) * 2 + core},
        )

    def late_copy(i, u=0, size=size):
        at = pl.ds(i * per + u, size)
        return remote(
            lsend.at[at], lrecv.at[at], l_send.at[i + u], l_recv.at[i + u], {"section": sec - 1}
        )

    def compute(i):
        wg_copy(i).wait()
        wu_copy(i).wait()
        w = wg_v[unit(i)].reshape(size * wc, -1)
        back = lax.dot_general(dg_v[...], w, NT, preferred_element_type=F32)
        w = wu_v[unit(i)].reshape(size * wc, -1)
        back = back + lax.dot_general(du_v[...], w, NT, preferred_element_type=F32)
        for j in range(size):
            piece = back[:, j * wc : (j + 1) * wc]
            psend[i * size + j] = piece[half:].astype(BF16).reshape(chips, blk, wc)
            keep[i * size + j] = piece[:half].reshape(chips, blk, wc)
        pair_copy(i).start()

    def chip_sum(i, group=size):
        pair_copy(i).wait_recv()
        for u in range(0, size, group):
            for k in range(1, chips):
                other = lax.rem(chip + k, chips)
                for j in range(u, u + group):
                    at = i * size + j
                    ysend[k - 1, at] = (keep[at, other] + precv[at, other].astype(F32)).astype(BF16)
                y_copy(i, k, u, group).start()

    def finish(i, group=size):
        for u in range(0, size, group):
            for k in range(1, chips):
                y_copy(i, k, u, group).wait_recv()
            for j in range(u, u + group):
                at = i * size + j
                total = keep[at, chip] + precv[at, chip].astype(F32)
                for k in range(1, chips):
                    total = total + yrecv[k - 1, at].astype(F32)
                lsend[at] = (late_v[at].astype(F32) + jnp.concatenate([wcol_v[...]] * (wc // 128), axis=1) * total).astype(BF16)

            @pl.when(has_prev)
            def _():
                late_copy(i, u, group).start()

    def drain(i, group=size):
        pair_copy(i).wait_send()
        for u in range(0, size, group):
            for k in range(1, chips):
                y_copy(i, k, u, group).wait_send()

    def landed(i, group=size):
        for u in range(0, size, group):
            @pl.when(has_prev)
            def _():
                late_copy(i, u, group).wait_send()

            @pl.when(has_next)
            def _():
                late_copy(i, u, group).wait_recv()

    lag = 3

    def body(i, carry):
        compute(i)

        @pl.when(i >= 1)
        def _():
            chip_sum(i - 1)

        @pl.when(i >= lag)
        def _():
            finish(i - lag)

        return carry

    lax.fori_loop(0, steps, body, 0)
    start_route()
    chip_sum(last, 1)
    for i in range(max(0, steps - lag), last):
        finish(i)
    end_route()
    route_store().start()
    sent_rows()
    for k in range(1, n):
        route_copy(k).wait_send()
    for i in range(last):
        drain(i)
    sent_early()
    finish(last, 1)
    drain(last, 1)
    route_store().wait()
    for i in range(last):
        landed(i)
    landed(last, 1)


def place(sections, cfg, late_v, early_v, pick_v, route_v, out_hbm, route_out, out_v, o_sem, s_sem):
    micro, tok, cap, pw, npw, wc = cfg
    per = pw // wc
    spare = tok - cap
    keep = lax.axis_index("section") < sections - 1
    c_route = pltpu.make_async_copy(route_v, route_out, s_sem)
    c_route.start()

    def store(c):
        cols = slice(c * pw, (c + 1) * pw)
        return pltpu.make_async_copy(out_v.at[:, :, cols], out_hbm.at[:, :, cols], o_sem.at[c])

    for c in range(npw):
        for m in range(micro):
            for j in range(c * per, (c + 1) * per):
                cols = slice(j * wc, (j + 1) * wc)
                mixed = jnp.concatenate(
                    [late_v[j, m * cap : (m + 1) * cap], early_v[m * spare : (m + 1) * spare, cols]],
                    axis=0,
                )
                mixed = lax.dot_general(pick_v[m], mixed, TN, preferred_element_type=F32)
                out_v[m, :, cols] = jnp.where(keep, mixed, 0.0).astype(BF16)
        store(c).start()
    for c in range(npw):
        store(c).wait()
    c_route.wait()


def solution(mesh):
    sections = mesh.shape["section"]
    n = mesh.shape["fsdp"]

    def local(out_grad, expert_ids, route_weight, gate_pre, up_pre, w_gate, w_up, w_down):
        micro, tok, width = out_grad.shape[1:]
        cap = gate_pre.shape[2] // n
        ff = gate_pre.shape[3]
        chips = n // 2
        blk = micro * cap
        rows = n * blk
        spare = tok - cap
        cuts = blocks(width, 512)
        wc = split(width, 256)
        fw = split(ff, 512)
        nd, nc, nf = len(cuts), width // wc, ff // fw
        np_ = len(spans(nc))
        cfg = (micro, tok, cap, cuts, wc, nc, fw, nf)
        any_spec = pl.BlockSpec(memory_space=pl.ANY)
        vm = pltpu.VMEM
        dma = pltpu.SemaphoreType.DMA
        late, early, pick, route = pl.pallas_call(
            functools.partial(kernel, sections, n, cfg),
            out_shape=(
                vm((nc, blk, wc), BF16),
                vm((micro * spare, width), BF16),
                vm((micro, tok, tok), BF16),
                vm((micro, tok), F32),
            ),
            in_specs=[any_spec] * 8,
            out_specs=(any_spec,) * 4,
            scratch_shapes=[
                vm((micro, tok, width), BF16),
                vm((micro, expert_ids.shape[3], tok), jnp.int32),
                vm((micro, tok), BF16),
                vm((2, chips, micro, cap, ff), BF16),
                vm((2, chips, micro, cap, ff), BF16),
                vm((nc, wc, ff), BF16),
                vm((nc, wc, ff), BF16),
                vm((ff, width), BF16),
                vm((2, chips, blk, width), BF16),
                vm((nc, blk, wc), BF16),
                vm((micro * spare, width), BF16),
                vm((micro, tok, tok), BF16),
                vm((blk, 128), F32),
                vm((n * micro, cap, ff), F32),
                vm((n * micro, cap, ff), F32),
                vm((nf, rows, fw), F32),
                vm((rows, ff), BF16),
                vm((rows, ff), BF16),
                vm((rows, 128), F32),
                vm((n, 8, 128), F32),
                vm((n, 8, 128), F32),
                vm((micro, tok), F32),
                vm((nc, chips, blk, wc), BF16),
                vm((nc, chips, blk, wc), BF16),
                vm((nc, chips, blk, wc), F32),
                vm((chips - 1, nc, blk, wc), BF16),
                vm((chips - 1, nc, blk, wc), BF16),
                vm((nc, blk, wc), BF16),
                dma((4,)),
                dma((2 * micro,)), dma((2 * micro,)),
                dma((nd,)), dma((np_,)), dma((np_,)),
                dma((nd, chips)), dma((nd, chips)),
                dma((nd,)), dma((nd,)),
                dma((nd, chips)), dma((nd, chips)),
                dma((np_,)), dma((np_,)),
                dma((np_ + 1, chips)), dma((np_ + 1, chips)),
                dma((np_ + 1,)), dma((np_ + 1,)),
                dma, dma, dma, dma,
                dma((n,)), dma((n,)),
            ],
            compiler_params=pltpu.CompilerParams(
                collective_id=0, has_side_effects=True, vmem_limit_bytes=62914560
            ),
        )(
            out_grad[0],
            jnp.swapaxes(expert_ids[0], 1, 2),
            route_weight[0],
            gate_pre[0].reshape(micro, chips, 2, cap, ff),
            up_pre[0].reshape(micro, chips, 2, cap, ff),
            w_gate[0].reshape(nc, wc, ff),
            w_up[0].reshape(nc, wc, ff),
            w_down[0],
        )
        late, early, pick, route = (
            pltpu.with_memory_space_constraint(x, pltpu.VMEM) for x in (late, early, pick, route)
        )
        pw = split(width, 1024)
        npw = width // pw
        prev, route = pl.pallas_call(
            functools.partial(place, sections, (micro, tok, cap, pw, npw, wc)),
            out_shape=(
                jax.ShapeDtypeStruct((micro, tok, width), BF16),
                jax.ShapeDtypeStruct((micro, tok), F32),
            ),
            in_specs=[pl.BlockSpec(memory_space=pltpu.VMEM)] * 4,
            out_specs=(any_spec, any_spec),
            scratch_shapes=[vm((micro, tok, width), BF16), dma((npw,)), dma],
        )(late, early, pick, route)
        return prev[None], route[None]

    return jax.shard_map(
        local,
        mesh=mesh,
        in_specs=(
            P("section", None, "fsdp", None),
            P("section", None, "fsdp", None),
            P("section", None, "fsdp"),
            P("section", None, None, "fsdp"),
            P("section", None, None, "fsdp"),
            P("section", None, "fsdp"),
            P("section", None, "fsdp"),
            P("section", "fsdp", None),
        ),
        out_specs=(P("section", None, "fsdp", None), P("section", None, "fsdp")),
        check_vma=False,
    )
```

```python
import functools

import jax
import jax.numpy as jnp
from jax import lax
from jax.experimental import pallas as pl
from jax.experimental.pallas import tpu as pltpu
from jax.sharding import PartitionSpec as P

MESH = pl.DeviceIdType.MESH
F32 = jnp.float32
BF16 = jnp.bfloat16
NT = (((1,), (1,)), ((), ()))
TN = (((0,), (0,)), ((), ()))
window_expert = 0
LASTW = 128
DIRECT = 1


def split(total, most):
    best = 128
    for width in range(128, most + 1, 128):
        if total % width == 0:
            best = width
    return best


def blocks(total, most):
    width = split(total, most)
    out = [(at, width) for at in range(0, total, width)]
    if LASTW and width > LASTW:
        at, _ = out.pop()
        out += [(at, width - LASTW), (at + width - LASTW, LASTW)]
    return out


def spans(units):
    size = 2 if units % 2 == 0 else 1
    return [(at, size) for at in range(0, units, size)]


def kernel(
    sections, n, cfg,
    dy_hbm, ids_hbm, wt_hbm, gate_hbm, up_hbm, wg_hbm, wu_hbm, wd_hbm,
    lrecv, early_r, pick_r, route_out,
    dy_v, ids_v, wt_v, gate_v, up_v, wg_v, wu_v, wd_v,
    rows_v, late_v, early_v, pick_v, wcol_v,
    a_v, b_v, q_v, dg_v, du_v, racc_v, rsend_v, rrecv_v, route_v,
    psend, precv, keep, ysend, yrecv, lsend,
    in_sem, g_sem, u_sem, wd_sem, wg_sem, wu_sem,
    gy_send, gy_recv, gp_send, gp_recv, rl_send, rl_recv,
    p_send, p_recv, y_send, y_recv, l_send, l_recv,
    e_send, e_recv, k_send, k_recv, r_send, r_recv,
):
    micro, tok, cap, cuts, wc, nc, fw, nf = cfg
    nd = len(cuts)
    chips = n // 2
    blk = micro * cap
    rows = n * blk
    half = chips * blk
    spare = tok - cap
    parts = spans(nc)
    steps = len(parts)
    size = parts[0][1]
    per = size
    last = steps - 1
    sec = lax.axis_index("section")
    me = lax.axis_index("fsdp")
    core = lax.rem(me, 2)
    chip = me // 2
    partner = chip * 2 + (1 - core)
    has_prev = sec > 0
    has_next = sec < sections - 1

    def local(src, dst, sem):
        return pltpu.make_async_copy(src, dst, sem)

    def remote(src, dst, ssem, rsem, to):
        return pltpu.make_async_remote_copy(
            src_ref=src, dst_ref=dst, send_sem=ssem, recv_sem=rsem,
            device_id=to, device_id_type=MESH,
        )

    c_ids = local(ids_hbm, ids_v, in_sem.at[0])
    c_wt = local(wt_hbm, wt_v, in_sem.at[1])
    c_dy = local(dy_hbm, dy_v, in_sem.at[2])
    c_ids.start()
    c_dy.start()
    c_wt.start()

    barrier = pltpu.get_barrier_semaphore()
    for k in range(1, n):
        pl.semaphore_signal(
            barrier, inc=1, device_id={"fsdp": lax.rem(me + k, n)}, device_id_type=MESH
        )

    @pl.when(has_prev)
    def _():
        pl.semaphore_signal(barrier, inc=1, device_id={"section": sec - 1}, device_id_type=MESH)

    @pl.when(has_next)
    def _():
        pl.semaphore_signal(barrier, inc=1, device_id={"section": sec + 1}, device_id_type=MESH)

    c_gate = []
    c_up = []
    for m in range(micro):
        for r in range(2):
            side = core if r == 0 else 1 - core
            at = m * 2 + r
            c_gate.append(local(gate_hbm.at[m, :, side], gate_v.at[r, :, m], g_sem.at[at]))
            c_up.append(local(up_hbm.at[m, :, side], up_v.at[r, :, m], u_sem.at[at]))

    def cut(d):
        at, size = cuts[d]
        return slice(at, at + size)

    def wd_copy(d):
        return local(wd_hbm.at[:, cut(d)], wd_v.at[:, cut(d)], wd_sem.at[d])

    def unit(i):
        return pl.ds(i * size, size)

    def wg_copy(i):
        return local(wg_hbm.at[unit(i)], wg_v.at[unit(i)], wg_sem.at[i])

    def wu_copy(i):
        return local(wu_hbm.at[unit(i)], wu_v.at[unit(i)], wu_sem.at[i])

    t_row = lax.broadcasted_iota(jnp.int32, (tok, tok), 0)
    t_col = lax.broadcasted_iota(jnp.int32, (tok, tok), 1)
    before = (t_row < t_col).astype(BF16)
    every = jnp.ones((tok, tok), BF16)
    lane = lax.broadcasted_iota(jnp.int32, (1, tok), 1).astype(F32)
    row_f = t_row.astype(F32)
    c_ids.wait()
    routeds, orders, counts, takes = [], [], [], []
    for m in range(micro):
        routed = jnp.max((ids_v[m] == window_expert).astype(F32), axis=0, keepdims=True)
        r8 = jnp.broadcast_to(routed, (8, tok)).astype(BF16)
        order = jnp.dot(r8, before, preferred_element_type=F32)[0:1]
        routeds.append(routed)
        orders.append(order)
        takes.append(jnp.where(row_f[:cap] == order, routed, 0.0))
    takes_b = [take.astype(BF16) for take in takes]
    c_dy.wait()

    def rows_at(r, c, d):
        return rows_v.at[r, c, :, cut(d)]

    def y_rows(d, k, owner):
        return remote(
            rows_at(0, owner, d), rows_at(0, owner, d), gy_send.at[d, k], gy_recv.at[d, owner],
            {"fsdp": lax.rem(chip + k, chips) * 2 + core},
        )

    def cross_rows(d, k):
        return remote(
            rows_at(0, chip, d), rows_at(1, chip, d), rl_send.at[d, k], rl_recv.at[d, chip],
            {"fsdp": lax.rem(chip + k, chips) * 2 + 1 - core},
        )

    def relay_rows(d, k):
        other = lax.rem(chip + k, chips)
        return remote(
            rows_at(0, other, d), rows_at(1, other, d), rl_send.at[d, k], rl_recv.at[d, other],
            {"fsdp": partner},
        )

    def pair_rows(d):
        return remote(
            rows_at(0, chip, d), rows_at(1, chip, d), gp_send.at[d], gp_recv.at[d],
            {"fsdp": partner},
        )

    def straight(d):
        return DIRECT and d == nd - 1

    def send_rows(d):
        for k in range(1, chips):
            y_rows(d, k, chip).start()
            if straight(d):
                cross_rows(d, k).start()
        pair_rows(d).start()

    for d in range(nd):
        cols = cut(d)
        for m in range(micro):
            rows_v[0, chip, m * cap : (m + 1) * cap, cols] = jnp.dot(
                takes_b[m], dy_v[m, :, cols], preferred_element_type=F32
            ).astype(BF16)
        if d == 0:
            wd_copy(0).start()
            pl.semaphore_wait(
                barrier, n - 1 + has_prev.astype(jnp.int32) + has_next.astype(jnp.int32)
            )
        send_rows(d)
        if d == 0:
            for copy in c_gate + c_up:
                copy.start()
        if d > 0:
            wd_copy(d).start()
    for i in range(len(parts)):
        wg_copy(i).start()
        wu_copy(i).start()

    def early_copy():
        return remote(early_v, early_r, e_send, e_recv, {"section": sec - 1})

    def pick_copy():
        return remote(pick_v, pick_r, k_send, k_recv, {"section": sec - 1})

    c_wt.wait()
    picks = []
    for m in range(micro):
        routed, order = routeds[m], orders[m]
        r8 = jnp.broadcast_to(routed, (8, tok)).astype(BF16)
        count = jnp.dot(r8, every, preferred_element_type=F32)[0:1]
        free = lane - order
        slot = jnp.where(
            routed > 0.5, order, jnp.where(free < spare, cap + free, count + free - spare)
        )
        pick = (slot == row_f).astype(BF16)
        w_row = wt_v[m : m + 1, :].astype(F32)
        wcol_v[m * cap : (m + 1) * cap, :] = jnp.broadcast_to(
            jnp.sum(takes[m] * w_row, axis=1, keepdims=True), (cap, 128)
        )
        pick_v[m] = pick
        picks.append(pick)
    for m in range(micro):
        for j in range(nc):
            cols = slice(j * wc, (j + 1) * wc)
            mix = jnp.dot(picks[m], dy_v[m, :, cols], preferred_element_type=F32)
            late_v[j, m * cap : (m + 1) * cap, :] = mix[:cap].astype(BF16)
            early_v[m * spare : (m + 1) * spare, cols] = mix[cap:].astype(BF16)

    @pl.when(has_prev)
    def _():
        pick_copy().start()
        early_copy().start()

    for copy in c_gate + c_up:
        copy.wait()

    def terms(i, carry):
        r = i // (chips * micro)
        j = lax.rem(i, chips * micro)
        at = j // micro
        m = lax.rem(j, micro)
        g = gate_v[r, at, m].astype(F32)
        u = up_v[r, at, m].astype(F32)
        sg = 1.0 / (1.0 + jnp.exp(-g))
        a_v[i] = u * sg * (1.0 + g * (1.0 - sg))
        b_v[i] = g * sg
        return carry

    lax.fori_loop(0, n * micro, terms, 0)

    def relay(d):
        for k in range(1, chips):
            y_rows(d, k, lax.rem(chip + k, chips)).wait_recv()
            if not straight(d):
                relay_rows(d, k).start()

    def relayed(d):
        pair_rows(d).wait_recv()
        for k in range(1, chips):
            relay_rows(d, k).wait_recv()

    def sent_rows():
        for d in range(nd):
            pair_rows(d).wait_send()
            for k in range(1, chips):
                y_rows(d, k, chip).wait_send()
                if straight(d):
                    cross_rows(d, k).wait_send()
                else:
                    relay_rows(d, k).wait_send()

    def sent_early():
        @pl.when(has_prev)
        def _():
            pick_copy().wait_send()
            early_copy().wait_send()

        @pl.when(has_next)
        def _():
            pick_copy().wait_recv()
            early_copy().wait_recv()

    relay(0)
    for d in range(nd):
        if d + 1 < nd:
            relay(d + 1)
        wd_copy(d).wait()
        relayed(d)
        x = rows_v[:, :, :, cut(d)].reshape(rows, cuts[d][1])
        if d + 1 < nd:
            for f in range(nf):
                part = lax.dot_general(
                    x, wd_v[f * fw : (f + 1) * fw, cut(d)], NT, preferred_element_type=F32
                )
                if d == 0:
                    q_v[f] = part
                else:
                    q_v[f] += part
        else:
            route = jnp.zeros((rows, 128), F32)
            for f in range(nf):
                cols = slice(f * fw, (f + 1) * fw)
                q = lax.dot_general(x, wd_v[cols, cut(d)], NT, preferred_element_type=F32)
                if nd > 1:
                    q = q + q_v[f]
                d_up = q * b_v[:, :, cols].reshape(rows, fw)
                u = up_v[:, :, :, :, cols].reshape(rows, fw).astype(F32)
                dg_v[:, cols] = (q * a_v[:, :, cols].reshape(rows, fw)).astype(BF16)
                du_v[:, cols] = d_up.astype(BF16)
                term = d_up * u
                for j in range(fw // 128):
                    route = route + term[:, j * 128 : (j + 1) * 128]
            racc_v[...] = route

    eye = (
        lax.broadcasted_iota(jnp.int32, (blk, 128), 0)
        == lax.broadcasted_iota(jnp.int32, (blk, 128), 1)
    ).astype(F32)

    def route_copy(k):
        return remote(
            rsend_v.at[k], rrecv_v.at[k], r_send.at[k], r_recv.at[k],
            {"fsdp": lax.rem(me + k, n)},
        )

    def start_route():
        sums = jnp.sum(racc_v[...], axis=1, keepdims=True)
        racc_v[...] = jnp.broadcast_to(sums, (rows, 128))
        for k in range(n):
            to = lax.rem(me + k, n)
            side = lax.rem(to + core, 2)
            first = pl.multiple_of((side * chips + to // 2) * blk, blk)
            row = jnp.sum(racc_v[pl.ds(first, blk)] * eye, axis=0, keepdims=True)
            rsend_v[k] = jnp.broadcast_to(row, (8, 128))
        for k in range(1, n):
            route_copy(k).start()

    def end_route():
        total = rsend_v[0]
        for k in range(1, n):
            route_copy(k).wait_recv()
            total = total + rrecv_v[k]
        col = jnp.sum(eye * total[0:1], axis=1, keepdims=True)
        for m in range(micro):
            route_v[m : m + 1, :] = jnp.sum(
                takes[m] * col[m * cap : (m + 1) * cap], axis=0, keepdims=True
            )

    def route_store():
        return local(route_v, route_out, in_sem.at[3])

    def pair_copy(i):
        return remote(
            psend.at[unit(i)], precv.at[unit(i)], p_send.at[i], p_recv.at[i], {"fsdp": partner}
        )

    def y_copy(i, k, u=0, size=size):
        at = pl.ds(i * per + u, size)
        return remote(
            ysend.at[k - 1, at], yrecv.at[k - 1, at], y_send.at[i + u, k], y_recv.at[i + u, k],
            {"fsdp": lax.rem(chip + k, chips) * 2 + core},
        )

    def late_copy(i, u=0, size=size):
        at = pl.ds(i * per + u, size)
        return remote(
            lsend.at[at], lrecv.at[at], l_send.at[i + u], l_recv.at[i + u], {"section": sec - 1}
        )

    def compute(i):
        wg_copy(i).wait()
        wu_copy(i).wait()
        w = wg_v[unit(i)].reshape(size * wc, -1)
        back = lax.dot_general(dg_v[...], w, NT, preferred_element_type=F32)
        w = wu_v[unit(i)].reshape(size * wc, -1)
        back = back + lax.dot_general(du_v[...], w, NT, preferred_element_type=F32)
        for j in range(size):
            piece = back[:, j * wc : (j + 1) * wc]
            psend[i * size + j] = piece[half:].astype(BF16).reshape(chips, blk, wc)
            keep[i * size + j] = piece[:half].reshape(chips, blk, wc)
        pair_copy(i).start()

    def chip_sum(i, group=size):
        pair_copy(i).wait_recv()
        for u in range(0, size, group):
            for k in range(1, chips):
                other = lax.rem(chip + k, chips)
                for j in range(u, u + group):
                    at = i * size + j
                    ysend[k - 1, at] = (keep[at, other] + precv[at, other].astype(F32)).astype(BF16)
                y_copy(i, k, u, group).start()

    def finish(i, group=size):
        for u in range(0, size, group):
            for k in range(1, chips):
                y_copy(i, k, u, group).wait_recv()
            for j in range(u, u + group):
                at = i * size + j
                total = keep[at, chip] + precv[at, chip].astype(F32)
                for k in range(1, chips):
                    total = total + yrecv[k - 1, at].astype(F32)
                lsend[at] = (late_v[at].astype(F32) + jnp.concatenate([wcol_v[...]] * (wc // 128), axis=1) * total).astype(BF16)

            @pl.when(has_prev)
            def _():
                late_copy(i, u, group).start()

    def drain(i, group=size):
        pair_copy(i).wait_send()
        for u in range(0, size, group):
            for k in range(1, chips):
                y_copy(i, k, u, group).wait_send()

    def landed(i, group=size):
        for u in range(0, size, group):
            @pl.when(has_prev)
            def _():
                late_copy(i, u, group).wait_send()

            @pl.when(has_next)
            def _():
                late_copy(i, u, group).wait_recv()

    lag = 3

    def body(i, carry):
        compute(i)

        @pl.when(i >= 1)
        def _():
            chip_sum(i - 1)

        @pl.when(i >= lag)
        def _():
            finish(i - lag)

        return carry

    lax.fori_loop(0, steps, body, 0)
    start_route()
    chip_sum(last, 1)
    for i in range(max(0, steps - lag), last):
        finish(i)
    end_route()
    route_store().start()
    sent_rows()
    for k in range(1, n):
        route_copy(k).wait_send()
    for i in range(last):
        drain(i)
    sent_early()
    finish(last, 1)
    drain(last, 1)
    route_store().wait()
    for i in range(last):
        landed(i)
    landed(last, 1)


def place(sections, cfg, late_v, early_v, pick_v, route_v, out_hbm, route_out, out_v, o_sem, s_sem):
    micro, tok, cap, pw, npw, wc = cfg
    per = pw // wc
    spare = tok - cap
    keep = lax.axis_index("section") < sections - 1
    c_route = pltpu.make_async_copy(route_v, route_out, s_sem)
    c_route.start()

    def store(c):
        cols = slice(c * pw, (c + 1) * pw)
        return pltpu.make_async_copy(out_v.at[:, :, cols], out_hbm.at[:, :, cols], o_sem.at[c])

    for c in range(npw):
        for m in range(micro):
            for j in range(c * per, (c + 1) * per):
                cols = slice(j * wc, (j + 1) * wc)
                mixed = jnp.concatenate(
                    [late_v[j, m * cap : (m + 1) * cap], early_v[m * spare : (m + 1) * spare, cols]],
                    axis=0,
                )
                mixed = lax.dot_general(pick_v[m], mixed, TN, preferred_element_type=F32)
                out_v[m, :, cols] = jnp.where(keep, mixed, 0.0).astype(BF16)
        store(c).start()
    for c in range(npw):
        store(c).wait()
    c_route.wait()


def solution(mesh):
    sections = mesh.shape["section"]
    n = mesh.shape["fsdp"]

    def local(out_grad, expert_ids, route_weight, gate_pre, up_pre, w_gate, w_up, w_down):
        micro, tok, width = out_grad.shape[1:]
        cap = gate_pre.shape[2] // n
        ff = gate_pre.shape[3]
        chips = n // 2
        blk = micro * cap
        rows = n * blk
        spare = tok - cap
        cuts = blocks(width, 768)
        wc = split(width, 256)
        fw = split(ff, 512)
        nd, nc, nf = len(cuts), width // wc, ff // fw
        np_ = len(spans(nc))
        cfg = (micro, tok, cap, cuts, wc, nc, fw, nf)
        any_spec = pl.BlockSpec(memory_space=pl.ANY)
        vm = pltpu.VMEM
        dma = pltpu.SemaphoreType.DMA
        late, early, pick, route = pl.pallas_call(
            functools.partial(kernel, sections, n, cfg),
            out_shape=(
                vm((nc, blk, wc), BF16),
                vm((micro * spare, width), BF16),
                vm((micro, tok, tok), BF16),
                vm((micro, tok), F32),
            ),
            in_specs=[any_spec] * 8,
            out_specs=(any_spec,) * 4,
            scratch_shapes=[
                vm((micro, tok, width), BF16),
                vm((micro, expert_ids.shape[3], tok), jnp.int32),
                vm((micro, tok), BF16),
                vm((2, chips, micro, cap, ff), BF16),
                vm((2, chips, micro, cap, ff), BF16),
                vm((nc, wc, ff), BF16),
                vm((nc, wc, ff), BF16),
                vm((ff, width), BF16),
                vm((2, chips, blk, width), BF16),
                vm((nc, blk, wc), BF16),
                vm((micro * spare, width), BF16),
                vm((micro, tok, tok), BF16),
                vm((blk, 128), F32),
                vm((n * micro, cap, ff), F32),
                vm((n * micro, cap, ff), F32),
                vm((nf, rows, fw), F32),
                vm((rows, ff), BF16),
                vm((rows, ff), BF16),
                vm((rows, 128), F32),
                vm((n, 8, 128), F32),
                vm((n, 8, 128), F32),
                vm((micro, tok), F32),
                vm((nc, chips, blk, wc), BF16),
                vm((nc, chips, blk, wc), BF16),
                vm((nc, chips, blk, wc), F32),
                vm((chips - 1, nc, blk, wc), BF16),
                vm((chips - 1, nc, blk, wc), BF16),
                vm((nc, blk, wc), BF16),
                dma((4,)),
                dma((2 * micro,)), dma((2 * micro,)),
                dma((nd,)), dma((np_,)), dma((np_,)),
                dma((nd, chips)), dma((nd, chips)),
                dma((nd,)), dma((nd,)),
                dma((nd, chips)), dma((nd, chips)),
                dma((np_,)), dma((np_,)),
                dma((np_ + 1, chips)), dma((np_ + 1, chips)),
                dma((np_ + 1,)), dma((np_ + 1,)),
                dma, dma, dma, dma,
                dma((n,)), dma((n,)),
            ],
            compiler_params=pltpu.CompilerParams(
                collective_id=0, has_side_effects=True, vmem_limit_bytes=62914560
            ),
        )(
            out_grad[0],
            jnp.swapaxes(expert_ids[0], 1, 2),
            route_weight[0],
            gate_pre[0].reshape(micro, chips, 2, cap, ff),
            up_pre[0].reshape(micro, chips, 2, cap, ff),
            w_gate[0].reshape(nc, wc, ff),
            w_up[0].reshape(nc, wc, ff),
            w_down[0],
        )
        late, early, pick, route = (
            pltpu.with_memory_space_constraint(x, pltpu.VMEM) for x in (late, early, pick, route)
        )
        pw = split(width, 1024)
        npw = width // pw
        prev, route = pl.pallas_call(
            functools.partial(place, sections, (micro, tok, cap, pw, npw, wc)),
            out_shape=(
                jax.ShapeDtypeStruct((micro, tok, width), BF16),
                jax.ShapeDtypeStruct((micro, tok), F32),
            ),
            in_specs=[pl.BlockSpec(memory_space=pltpu.VMEM)] * 4,
            out_specs=(any_spec, any_spec),
            scratch_shapes=[vm((micro, tok, width), BF16), dma((npw,)), dma],
        )(late, early, pick, route)
        return prev[None], route[None]

    return jax.shard_map(
        local,
        mesh=mesh,
        in_specs=(
            P("section", None, "fsdp", None),
            P("section", None, "fsdp", None),
            P("section", None, "fsdp"),
            P("section", None, None, "fsdp"),
            P("section", None, None, "fsdp"),
            P("section", None, "fsdp"),
            P("section", None, "fsdp"),
            P("section", "fsdp", None),
        ),
        out_specs=(P("section", None, "fsdp", None), P("section", None, "fsdp")),
        check_vma=False,
    )
```
